256 devices in a mesh: blk: 8 (over y, core), wide: 32 (over x, z).
Axes of the slice: x: 4, y: 4, z: 8, core: 2. Of those that a mesh axis runs over, the one named last changes fastest.
Arguments:
- amplitudes: bfloat16 [2048, 262144], P(('blk', 'wide')), may hold values from -6 to 6
- integrals: bfloat16 [32, 256, 128, 128], P('wide', 'blk'), may hold values from -0.03125 to 0.03125
- out_tile: int32 [32, 256], P('wide'), may hold values from 0 to 31, as said below
- cd_slot: int32 [32, 256], P('wide'), may hold values from 0 to 63, as said below
Outputs:
- ladder: bfloat16 [2048, 4096], P('blk', 'wide')
The draws below stay inside these ranges and needn't reach their ends.
Inputs may be any that keep to these rules, and one draw needn't show every extreme that they name: `out_tile`: output tile a lies in sector a mod 8. In each group every one of its 64 contracted tiles appears in exactly 4 entries, once with each output tile of one sector, the sector drawn for that tile; entries are in no particular order. `cd_slot`: see out_tile.
All inputs are finite; a program needn't handle non-finite values.
Results may differ from the reference program's by a relative error of at most 0.001.
Values may be sent and summed in bfloat16 or wider, within the bound.
No kernel may reach another device: no remote copies, remote signals or barrier semaphores. Data moves between devices by JAX's collectives and lax.ppermute only.
A program may use at most 192 MiB of HBM per device.

```python
import math
import jax
import jax.numpy as jnp
from jax import lax

TILE = 128
SECTORS = 8
A_PER = 4
CG = 64
GROUPS = 32
KT = 2048
ENTRIES = 256
NIJ = 2048
N_WIDE = 32


def tile_lists(key):
    entries = CG * A_PER
    sectors = jax.random.randint(jax.random.fold_in(key, 11), (N_WIDE, CG), 0, SECTORS)
    slots = jnp.arange(entries, dtype=jnp.int32) // A_PER
    ranks = jnp.arange(entries, dtype=jnp.int32) % A_PER
    outputs = sectors[:, slots] + SECTORS * ranks[None, :]
    contracted = jnp.broadcast_to(slots[None, :], (N_WIDE, entries))
    group_keys = jax.random.split(jax.random.fold_in(key, 12), N_WIDE)
    orders = jax.vmap(lambda one_key: jax.random.permutation(one_key, entries))(group_keys)
    outputs = jnp.take_along_axis(outputs, orders, axis=1)
    contracted = jnp.take_along_axis(contracted, orders, axis=1)
    return (outputs.astype(jnp.int32), contracted.astype(jnp.int32))


def draw_out_tile(key, part):
    return tile_lists(key)[0]


def draw_cd_slot(key, part):
    return tile_lists(key)[1]


def levels(own_key, dims, shards, smallest, top_value):
    loudness = 1.0
    for axis_at, parts in shards:
        heights = jax.random.uniform(jax.random.fold_in(jax.random.fold_in(own_key, 6), axis_at), (parts,), jnp.float32, smallest / len(shards), top_value / len(shards))
        loudness = loudness * jnp.repeat(jnp.exp(heights), dims[axis_at] // parts).reshape((-1,) + (1,) * (len(dims) - 1 - axis_at))
    return loudness


def normal_values(rng, dims, spread, limit, shards=(), kind=jnp.bfloat16):
    loudness = levels(rng, dims, shards, -0.22, 0.18) if shards else 1.0
    result = jax.random.normal(rng, dims, jnp.float32) * spread * loudness
    return jnp.minimum(jnp.maximum(result, -limit), limit).astype(kind)


def setup_inputs(seed: int = 0) -> dict:
    streams_of = jax.random.split(jax.random.key(seed), 5)
    return {
        "amplitudes": normal_values(streams_of[0], (NIJ, KT * TILE), 1.0, 6.0, ((0, 256),)),
        "integrals": normal_values(streams_of[1], (GROUPS, ENTRIES, TILE, TILE), (KT * TILE // SECTORS) ** -0.5, 0.03125, ((0, 32), (1, 8))),
        "out_tile": draw_out_tile(jax.random.fold_in(streams_of[4], 71), 0),
        "cd_slot": draw_cd_slot(jax.random.fold_in(streams_of[4], 71), 0),
    }


def reference(amplitudes, integrals, out_tile, cd_slot):
    n_out = SECTORS * A_PER
    rows = amplitudes.shape[0]
    entries = CG * A_PER
    block = math.gcd(entries, 64)

    def group_step(total, group):
        start_col = group * (CG * TILE)
        columns = lax.dynamic_slice_in_dim(amplitudes, start_col, CG * TILE, 1).reshape(rows, CG, TILE)
        tiles = lax.dynamic_index_in_dim(integrals, group, 0, keepdims=False)
        outs = lax.dynamic_index_in_dim(out_tile, group, 0, keepdims=False)
        slots = lax.dynamic_index_in_dim(cd_slot, group, 0, keepdims=False)

        def block_step(accum, index):
            first = index * block
            tile_block = lax.dynamic_slice_in_dim(tiles, first, block, 0).astype(jnp.float32)
            out_block = lax.dynamic_slice_in_dim(outs, first, block, 0)
            slot_block = lax.dynamic_slice_in_dim(slots, first, block, 0)
            picked = jnp.take(columns, slot_block, axis=1).astype(jnp.float32)
            products = jnp.einsum("rkt,ktu->rku", picked, tile_block, precision=lax.Precision.HIGHEST)
            return accum.at[:, out_block, :].add(products), None

        total, _ = lax.scan(block_step, total, jnp.arange(entries // block, dtype=jnp.int32))
        return total, None

    total = jnp.zeros((rows, n_out, TILE), jnp.float32)
    total, _ = lax.scan(group_step, total, jnp.arange(GROUPS, dtype=jnp.int32))
    return total.reshape(rows, n_out * TILE).astype(jnp.bfloat16)
```

```python
import functools

import jax
import jax.numpy as jnp
from jax import lax
from jax.experimental import pallas as pl
from jax.experimental.pallas import tpu as pltpu
from jax.sharding import Mesh
from jax.sharding import PartitionSpec as P

SECTORS = 8
A_PER = 4
TILE = 128
SLOTS = 64
ENTRIES = SLOTS * A_PER
PAIRS = (SLOTS + SECTORS) // 2
PAD_SLOTS = 2 * PAIRS
N_OUT = SECTORS * A_PER
ROWS = 256
CODE_ROWS = ROWS + 16
STEP_PAIRS = 4
STEPS = PAIRS // STEP_PAIRS
TOP = 32760.0
TINY = 1e-30
GRAIN = 64.0


def tables(out_tile, cd_slot, y, c):
    entry = jnp.arange(ENTRIES, dtype=jnp.int32)
    key = cd_slot * A_PER + out_tile // SECTORS
    hit = key[None, :] == entry[:, None]
    where_entry = jnp.sum(jnp.where(hit, entry[None, :], 0), axis=1)
    source = where_entry // (ENTRIES // 8)
    hop = (y - source // 2) % 4
    other = jnp.where(source % 2 == c, 0, 1)
    place = ((other * 4 + hop) * (ENTRIES // 8) + where_entry % (ENTRIES // 8)).reshape(SLOTS, A_PER)
    sector = jnp.sum(jnp.where(hit, out_tile[None, :] % SECTORS, 0), axis=1).reshape(SLOTS, A_PER)[:, 0]
    slot = jnp.arange(SLOTS, dtype=jnp.int32)
    of_sector = sector[None, :] == jnp.arange(SECTORS, dtype=jnp.int32)[:, None]
    padded = (jnp.sum(of_sector.astype(jnp.int32), axis=1) + 1) // 2 * 2
    before = jnp.arange(SECTORS)[None, :] < jnp.arange(SECTORS)[:, None]
    start = jnp.sum(jnp.where(before, padded[None, :], 0), axis=1)
    earlier = (sector[None, :] == sector[:, None]) & (slot[None, :] < slot[:, None])
    rank = jnp.sum(earlier.astype(jnp.int32), axis=1)
    position = jnp.sum(jnp.where(of_sector, start[:, None], 0), axis=0) + rank
    at = position[None, :] == jnp.arange(PAD_SLOTS, dtype=jnp.int32)[:, None]
    valid = jnp.sum(at.astype(jnp.int32), axis=1)
    order = jnp.sum(jnp.where(at, slot[None, :], 0), axis=1)
    order_place = jnp.sum(jnp.where(at[:, :, None], place[None, :, :], 0), axis=1)
    pair_first = 2 * jnp.arange(PAIRS, dtype=jnp.int32)
    pair_sector = jnp.sum((start[None, :] <= pair_first[:, None]).astype(jnp.int32), axis=1) - 1
    return order, valid, order_place.reshape(-1), pair_sector


def arrange_kernel(valid, place, a, b, c, d, out):
    j = pl.program_id(0)

    @pl.when(valid[j] == 1)
    def _():
        for r, ref in enumerate((a, b, c, d)):
            out[0, :, r * TILE : (r + 1) * TILE] = ref[0]

    @pl.when(valid[j] == 0)
    def _():
        out[...] = jnp.zeros_like(out)


def arrange(valid, place, everything):
    def spec(r):
        return pl.BlockSpec((1, TILE, TILE), lambda j, v, p: (p[j * A_PER + r], 0, 0))

    return pl.pallas_call(
        arrange_kernel,
        grid_spec=pltpu.PrefetchScalarGridSpec(
            num_scalar_prefetch=2,
            grid=(PAD_SLOTS,),
            in_specs=[spec(r) for r in range(A_PER)],
            out_specs=pl.BlockSpec((1, TILE, A_PER * TILE), lambda j, v, p: (j, 0, 0)),
        ),
        out_shape=jax.ShapeDtypeStruct((PAD_SLOTS, TILE, A_PER * TILE), jnp.bfloat16),
        cost_estimate=pl.CostEstimate(flops=0, bytes_accessed=2 * 9 * 2**20, transcendentals=0),
        name="arrange",
    )(valid, place, everything, everything, everything, everything)


def ladder_kernel(order, pair_sector, x, w, out, acc):
    step = pl.program_id(0)

    @pl.when(step == 0)
    def _():
        acc[...] = jnp.zeros_like(acc)

    for i in range(STEP_PAIRS):
        pair = step * STEP_PAIRS + i
        s = pair_sector[pair]
        first = pl.multiple_of(order[2 * pair] * TILE, TILE)
        second = pl.multiple_of(order[2 * pair + 1] * TILE, TILE)
        left = jnp.concatenate([x[:, pl.ds(first, TILE)], x[:, pl.ds(second, TILE)]], axis=1)
        right = w[2 * i : 2 * i + 2].reshape(2 * TILE, A_PER * TILE)
        acc[s] += jnp.dot(left, right, preferred_element_type=jnp.float32)

    @pl.when(step == STEPS - 1)
    def _():
        def encode(s, _):
            for r in range(A_PER):
                v = acc[s, :, r * TILE : (r + 1) * TILE]
                top = jnp.maximum(jnp.max(jnp.abs(v), axis=0, keepdims=True), TINY)
                level = jnp.ceil(jnp.log2(top) * GRAIN + 1.0)
                factor = TOP * jnp.exp2(-level * (1.0 / GRAIN))
                out[r * SECTORS + s, :ROWS, :] = jnp.round(v * factor).astype(jnp.int32).astype(jnp.int16)
                out[r * SECTORS + s, ROWS:, :] = jnp.broadcast_to(level.astype(jnp.int32), (16, TILE)).astype(jnp.int16)
            return 0

        lax.fori_loop(0, SECTORS, encode, 0)


def ladder_codes(order, pair_sector, x, w):
    return pl.pallas_call(
        ladder_kernel,
        grid_spec=pltpu.PrefetchScalarGridSpec(
            num_scalar_prefetch=2,
            grid=(STEPS,),
            in_specs=[
                pl.BlockSpec((ROWS, SLOTS * TILE), lambda j, o, p: (0, 0), pipeline_mode=pl.Buffered(1)),
                pl.BlockSpec((2 * STEP_PAIRS, TILE, A_PER * TILE), lambda j, o, p: (j, 0, 0)),
            ],
            out_specs=pl.BlockSpec((N_OUT, CODE_ROWS, TILE), lambda j, o, p: (0, 0, 0)),
            scratch_shapes=[pltpu.VMEM((SECTORS, ROWS, A_PER * TILE), jnp.float32)],
        ),
        out_shape=jax.ShapeDtypeStruct((N_OUT, CODE_ROWS, TILE), jnp.int16),
        cost_estimate=pl.CostEstimate(flops=2 * 36 * 256 * 256 * 512, bytes_accessed=16 * 2**20, transcendentals=0),
        name="ladder_codes",
    )(order, pair_sector, x, w)


def total_kernel(codes, out, acc):
    def add(w, _):
        level = codes[w, ROWS : ROWS + 16, :].astype(jnp.int32).astype(jnp.float32)[:1]
        scale = jnp.exp2(level * (1.0 / GRAIN)) * (1.0 / TOP)
        acc[...] += codes[w, :ROWS, :].astype(jnp.int32).astype(jnp.float32) * scale
        return 0

    acc[...] = jnp.zeros_like(acc)
    lax.fori_loop(0, N_OUT, add, 0)
    out[...] = acc[...].astype(jnp.bfloat16)


def total(codes):
    return pl.pallas_call(
        total_kernel,
        out_shape=jax.ShapeDtypeStruct((ROWS, TILE), jnp.bfloat16),
        scratch_shapes=[pltpu.VMEM((ROWS, TILE), jnp.float32)],
        name="total",
    )(codes)


def on_device(amplitudes, integrals, out_tile, cd_slot):
    y, c = lax.axis_index("y"), lax.axis_index("c")
    order, valid, place, pair_sector = tables(out_tile[0], cd_slot[0], y, c)
    mine = integrals[0]
    same_core = [mine] + [lax.ppermute(mine, "y", [(i, (i + d) % 4) for i in range(4)]) for d in (1, 2, 3)]
    same_core = jnp.concatenate(same_core, axis=0)
    other_core = lax.ppermute(same_core, "c", [(0, 1), (1, 0)])
    everything = jnp.concatenate([same_core, other_core], axis=0)
    w = arrange(valid, place, everything)
    exchanged = lax.all_to_all(amplitudes, ("x", "z"), split_axis=1, concat_axis=0, tiled=True)
    codes = ladder_codes(order, pair_sector, exchanged, w)
    codes = lax.all_to_all(codes, ("x", "z"), split_axis=0, concat_axis=0, tiled=True)
    return total(codes)


def solution(mesh):
    grid = Mesh(mesh.devices.reshape(4, 2, 4, 8), ("y", "c", "x", "z"))
    blk, wide = ("y", "c"), ("x", "z")
    in_specs = (P(blk + wide, None), P(wide, blk, None, None), P(wide, None), P(wide, None))
    return jax.shard_map(on_device, mesh=grid, in_specs=in_specs, out_specs=P(blk, wide), check_vma=False)
```

```python
import jax
import jax.numpy as jnp
from jax import lax
from jax.experimental import pallas as pl
from jax.experimental.pallas import tpu as pltpu
from jax.sharding import Mesh
from jax.sharding import PartitionSpec as P

SECTORS = 8
A_PER = 4
TILE = 128
SLOTS = 64
ENTRIES = SLOTS * A_PER
PAIRS = (SLOTS + SECTORS) // 2
PAD_SLOTS = 2 * PAIRS
ROWS = 256
CODE_ROWS = ROWS + 16
STEP_PAIRS = 4
STEPS = PAIRS // STEP_PAIRS
TOP = 32760.0
TINY = 1e-30
GRAIN = 64.0


def tables(out_tile, cd_slot, y, c):
    entry = jnp.arange(ENTRIES, dtype=jnp.int32)
    key = cd_slot * A_PER + out_tile // SECTORS
    hit = key[None, :] == entry[:, None]
    where_entry = jnp.sum(jnp.where(hit, entry[None, :], 0), axis=1)
    source = where_entry // (ENTRIES // 8)
    hop = (y - source // 2) % 4
    other = jnp.where(source % 2 == c, 0, 1)
    place = ((other * 4 + hop) * (ENTRIES // 8) + where_entry % (ENTRIES // 8)).reshape(SLOTS, A_PER)
    sector = jnp.sum(jnp.where(hit, out_tile[None, :] % SECTORS, 0), axis=1).reshape(SLOTS, A_PER)[:, 0]
    slot = jnp.arange(SLOTS, dtype=jnp.int32)
    of_sector = sector[None, :] == jnp.arange(SECTORS, dtype=jnp.int32)[:, None]
    padded = (jnp.sum(of_sector.astype(jnp.int32), axis=1) + 1) // 2 * 2
    before = jnp.arange(SECTORS)[None, :] < jnp.arange(SECTORS)[:, None]
    start = jnp.sum(jnp.where(before, padded[None, :], 0), axis=1)
    earlier = (sector[None, :] == sector[:, None]) & (slot[None, :] < slot[:, None])
    rank = jnp.sum(earlier.astype(jnp.int32), axis=1)
    position = jnp.sum(jnp.where(of_sector, start[:, None], 0), axis=0) + rank
    at = position[None, :] == jnp.arange(PAD_SLOTS, dtype=jnp.int32)[:, None]
    valid = jnp.sum(at.astype(jnp.int32), axis=1)
    order = jnp.sum(jnp.where(at, slot[None, :], 0), axis=1)
    order_place = jnp.sum(jnp.where(at[:, :, None], place[None, :, :], 0), axis=1)
    pair_first = 2 * jnp.arange(PAIRS, dtype=jnp.int32)
    pair_sector = jnp.sum((start[None, :] <= pair_first[:, None]).astype(jnp.int32), axis=1) - 1
    return order, valid, order_place.reshape(-1), pair_sector


def arrange_kernel(valid, place, same_core, other_core, out, held, sem):
    j = pl.program_id(0)

    @pl.when(j == 0)
    def _():
        half = ENTRIES // 2
        one = pltpu.make_async_copy(same_core, held.at[:half], sem.at[0])
        two = pltpu.make_async_copy(other_core, held.at[half:], sem.at[1])
        one.start()
        two.start()
        one.wait()
        two.wait()

    for i in range(2 * STEP_PAIRS):
        at = j * 2 * STEP_PAIRS + i

        @pl.when(valid[at] == 1)
        def _():
            for r in range(A_PER):
                out[i, :, r * TILE : (r + 1) * TILE] = held[place[at * A_PER + r]]

        @pl.when(valid[at] == 0)
        def _():
            out[i] = jnp.zeros((TILE, A_PER * TILE), out.dtype)


def arrange(valid, place, same_core, other_core):
    return pl.pallas_call(
        arrange_kernel,
        grid_spec=pltpu.PrefetchScalarGridSpec(
            num_scalar_prefetch=2,
            grid=(STEPS,),
            in_specs=[pl.BlockSpec(memory_space=pl.ANY)] * 2,
            out_specs=pl.BlockSpec((2 * STEP_PAIRS, TILE, A_PER * TILE), lambda j, v, p: (j, 0, 0)),
            scratch_shapes=[
                pltpu.VMEM((ENTRIES, TILE, TILE), jnp.bfloat16),
                pltpu.SemaphoreType.DMA((2,)),
            ],
        ),
        out_shape=jax.ShapeDtypeStruct((PAD_SLOTS, TILE, A_PER * TILE), jnp.bfloat16),
        cost_estimate=pl.CostEstimate(flops=0, bytes_accessed=2 * 9 * 2**20, transcendentals=0),
        name="arrange",
    )(valid, place, same_core, other_core)


def put_codes(out, v):
    top = jnp.maximum(jnp.max(jnp.abs(v), axis=0, keepdims=True), TINY)
    level = jnp.ceil(jnp.log2(top) * GRAIN + 1.0)
    factor = TOP * jnp.exp2(-level * (1.0 / GRAIN))
    out[:ROWS, :] = jnp.round(v * factor).astype(jnp.int32).astype(jnp.int16)
    out[ROWS:, :] = jnp.broadcast_to(level.astype(jnp.int32), (CODE_ROWS - ROWS, TILE)).astype(jnp.int16)


def get_codes(codes):
    level = codes[ROWS:, :].astype(jnp.int32).astype(jnp.float32)[:1]
    scale = jnp.exp2(level * (1.0 / GRAIN)) * (1.0 / TOP)
    return codes[:ROWS, :].astype(jnp.int32).astype(jnp.float32) * scale


def ladder_kernel(order, pair_sector, *refs):
    tiles, (w, out, acc) = refs[: 2 * STEP_PAIRS], refs[2 * STEP_PAIRS :]
    step = pl.program_id(0)

    @pl.when(step == 0)
    def _():
        acc[...] = jnp.zeros_like(acc)

    for i in range(STEP_PAIRS):
        s = pair_sector[step * STEP_PAIRS + i]
        left = jnp.concatenate([tiles[2 * i][...], tiles[2 * i + 1][...]], axis=1)
        right = w[2 * i : 2 * i + 2].reshape(2 * TILE, A_PER * TILE)
        acc[s] += jnp.dot(left, right, preferred_element_type=jnp.float32)

    @pl.when(step == STEPS - 1)
    def _():
        def encode(s, _):
            for r in range(A_PER):
                put_codes(out.at[r, s], acc[s, :, r * TILE : (r + 1) * TILE])
            return 0

        lax.fori_loop(0, SECTORS, encode, 0)


def ladder_codes(order, pair_sector, x, w):
    def tile(i):
        return pl.BlockSpec((ROWS, TILE), lambda j, o, p: (0, o[j * 2 * STEP_PAIRS + i]))

    return pl.pallas_call(
        ladder_kernel,
        grid_spec=pltpu.PrefetchScalarGridSpec(
            num_scalar_prefetch=2,
            grid=(STEPS,),
            in_specs=[tile(i) for i in range(2 * STEP_PAIRS)]
            + [pl.BlockSpec((2 * STEP_PAIRS, TILE, A_PER * TILE), lambda j, o, p: (j, 0, 0))],
            out_specs=pl.BlockSpec((A_PER, SECTORS, CODE_ROWS, TILE), lambda j, o, p: (0, 0, 0, 0)),
            scratch_shapes=[pltpu.VMEM((SECTORS, ROWS, A_PER * TILE), jnp.float32)],
        ),
        out_shape=jax.ShapeDtypeStruct((A_PER, SECTORS, CODE_ROWS, TILE), jnp.int16),
        cost_estimate=pl.CostEstimate(flops=2 * 36 * 256 * 256 * 512, bytes_accessed=16 * 2**20, transcendentals=0),
        name="ladder_codes",
    )(order, pair_sector, *[x] * (2 * STEP_PAIRS), w)


def recode_kernel(codes, out):
    put_codes(out.at[0], sum(get_codes(codes.at[i, 0]) for i in range(A_PER)))


def recode(codes):
    return pl.pallas_call(
        recode_kernel,
        grid=(SECTORS,),
        in_specs=[pl.BlockSpec((A_PER, 1, CODE_ROWS, TILE), lambda j: (0, j, 0, 0))],
        out_specs=pl.BlockSpec((1, CODE_ROWS, TILE), lambda j: (j, 0, 0)),
        out_shape=jax.ShapeDtypeStruct((SECTORS, CODE_ROWS, TILE), jnp.int16),
        name="recode",
    )(codes)


def total_kernel(codes, out):
    out[...] = sum(get_codes(codes.at[i]) for i in range(SECTORS)).astype(jnp.bfloat16)


def total(codes):
    return pl.pallas_call(total_kernel, out_shape=jax.ShapeDtypeStruct((ROWS, TILE), jnp.bfloat16), name="total")(codes)


def on_device(amplitudes, integrals, out_tile, cd_slot):
    y, c = lax.axis_index("y"), lax.axis_index("c")
    order, valid, place, pair_sector = tables(out_tile[0], cd_slot[0], y, c)
    mine = integrals[0]
    same_core = [mine] + [lax.ppermute(mine, "y", [(i, (i + d) % 4) for i in range(4)]) for d in (1, 2, 3)]
    same_core = jnp.concatenate(same_core, axis=0)
    other_core = lax.ppermute(same_core, "c", [(0, 1), (1, 0)])
    w = arrange(valid, place, same_core, other_core)
    exchanged = lax.all_to_all(amplitudes, ("x", "z"), split_axis=1, concat_axis=0, tiled=True)
    codes = ladder_codes(order, pair_sector, exchanged, w)
    codes = lax.all_to_all(codes, "x", split_axis=0, concat_axis=0, tiled=True)
    codes = lax.all_to_all(recode(codes), "z", split_axis=0, concat_axis=0, tiled=True)
    return total(codes)


def solution(mesh):
    grid = Mesh(mesh.devices.reshape(4, 2, 4, 8), ("y", "c", "x", "z"))
    blk, wide = ("y", "c"), ("x", "z")
    in_specs = (P(blk + wide, None), P(wide, blk, None, None), P(wide, None), P(wide, None))
    return jax.shard_map(on_device, mesh=grid, in_specs=in_specs, out_specs=P(blk, wide), check_vma=False)
```

```python
import jax
import jax.numpy as jnp
from jax import lax
from jax.experimental import pallas as pl
from jax.experimental.pallas import tpu as pltpu
from jax.sharding import Mesh
from jax.sharding import PartitionSpec as P

SECTORS = 8
A_PER = 4
TILE = 128
SLOTS = 64
ENTRIES = SLOTS * A_PER
PAIRS = (SLOTS + SECTORS) // 2
PAD_SLOTS = 2 * PAIRS
ROWS = 256
CODE_ROWS = ROWS + 16
STEP_PAIRS = 9
STEPS = PAIRS // STEP_PAIRS
AHEAD = 2
TOP = 32760.0
TINY = 1e-30
GRAIN = 64.0


def tables(out_tile, cd_slot, y, c):
    entry = jnp.arange(ENTRIES, dtype=jnp.int32)
    key = cd_slot * A_PER + out_tile // SECTORS
    hit = key[None, :] == entry[:, None]
    where_entry = jnp.sum(jnp.where(hit, entry[None, :], 0), axis=1)
    source = where_entry // (ENTRIES // 8)
    hop = (y - source // 2) % 4
    other = jnp.where(source % 2 == c, 0, 1)
    place = ((other * 4 + hop) * (ENTRIES // 8) + where_entry % (ENTRIES // 8)).reshape(SLOTS, A_PER)
    sector = jnp.sum(jnp.where(hit, out_tile[None, :] % SECTORS, 0), axis=1).reshape(SLOTS, A_PER)[:, 0]
    slot = jnp.arange(SLOTS, dtype=jnp.int32)
    of_sector = sector[None, :] == jnp.arange(SECTORS, dtype=jnp.int32)[:, None]
    padded = (jnp.sum(of_sector.astype(jnp.int32), axis=1) + 1) // 2 * 2
    before = jnp.arange(SECTORS)[None, :] < jnp.arange(SECTORS)[:, None]
    start = jnp.sum(jnp.where(before, padded[None, :], 0), axis=1)
    earlier = (sector[None, :] == sector[:, None]) & (slot[None, :] < slot[:, None])
    rank = jnp.sum(earlier.astype(jnp.int32), axis=1)
    position = jnp.sum(jnp.where(of_sector, start[:, None], 0), axis=0) + rank
    at = position[None, :] == jnp.arange(PAD_SLOTS, dtype=jnp.int32)[:, None]
    valid = jnp.sum(at.astype(jnp.int32), axis=1)
    order = jnp.sum(jnp.where(at, slot[None, :], 0), axis=1)
    order_place = jnp.sum(jnp.where(at[:, :, None], place[None, :, :], 0), axis=1)
    pair_first = 2 * jnp.arange(PAIRS, dtype=jnp.int32)
    pair_sector = jnp.sum((start[None, :] <= pair_first[:, None]).astype(jnp.int32), axis=1) - 1
    return order, valid, order_place.reshape(-1), pair_sector


def arrange_kernel(valid, place, same_core, other_core, out, held, sem):
    j = pl.program_id(0)

    @pl.when(j == 0)
    def _():
        half = ENTRIES // 2
        one = pltpu.make_async_copy(same_core, held.at[:half], sem.at[0])
        two = pltpu.make_async_copy(other_core, held.at[half:], sem.at[1])
        one.start()
        two.start()
        one.wait()
        two.wait()

    for i in range(2 * STEP_PAIRS):
        at = j * 2 * STEP_PAIRS + i

        @pl.when(valid[at] == 1)
        def _():
            for r in range(A_PER):
                out[i, :, r * TILE : (r + 1) * TILE] = held[place[at * A_PER + r]]

        @pl.when(valid[at] == 0)
        def _():
            out[i] = jnp.zeros((TILE, A_PER * TILE), out.dtype)


def arrange(valid, place, same_core, other_core):
    return pl.pallas_call(
        arrange_kernel,
        grid_spec=pltpu.PrefetchScalarGridSpec(
            num_scalar_prefetch=2,
            grid=(STEPS,),
            in_specs=[pl.BlockSpec(memory_space=pl.ANY)] * 2,
            out_specs=pl.BlockSpec((2 * STEP_PAIRS, TILE, A_PER * TILE), lambda j, v, p: (j, 0, 0)),
            scratch_shapes=[
                pltpu.VMEM((ENTRIES, TILE, TILE), jnp.bfloat16),
                pltpu.SemaphoreType.DMA((2,)),
            ],
        ),
        out_shape=jax.ShapeDtypeStruct((PAD_SLOTS, TILE, A_PER * TILE), jnp.bfloat16),
        cost_estimate=pl.CostEstimate(flops=0, bytes_accessed=2 * 9 * 2**20, transcendentals=0),
        name="arrange",
    )(valid, place, same_core, other_core)


def put_codes(out, v):
    top = jnp.maximum(jnp.max(jnp.abs(v), axis=0, keepdims=True), TINY)
    level = jnp.ceil(jnp.log2(top) * GRAIN + 1.0)
    factor = TOP * jnp.exp2(-level * (1.0 / GRAIN))
    out[:ROWS, :] = jnp.round(v * factor).astype(jnp.int32).astype(jnp.int16)
    out[ROWS:, :] = jnp.broadcast_to(level.astype(jnp.int32), (CODE_ROWS - ROWS, TILE)).astype(jnp.int16)


def get_codes(codes):
    level = codes[ROWS:, :].astype(jnp.int32).astype(jnp.float32)[:1]
    scale = jnp.exp2(level * (1.0 / GRAIN)) * (1.0 / TOP)
    return codes[:ROWS, :].astype(jnp.int32).astype(jnp.float32) * scale


def ladder_kernel(order, pair_sector, x_hbm, w_hbm, out, x, w, acc, x_sem, w_sem):
    x_copy = pltpu.make_async_copy(x_hbm, x, x_sem)
    x_copy.start()

    def w_copy(k):
        part = pl.ds(k * 2 * STEP_PAIRS, 2 * STEP_PAIRS)
        return pltpu.make_async_copy(w_hbm.at[part], w.at[part], w_sem.at[k])

    for k in range(AHEAD):
        w_copy(k).start()
    acc[...] = jnp.zeros_like(acc)
    x_copy.wait()

    def step(k, _):
        @pl.when(k + AHEAD < STEPS)
        def _():
            w_copy(k + AHEAD).start()

        w_copy(k).wait()
        for i in range(STEP_PAIRS):
            pair = k * STEP_PAIRS + i
            s = pair_sector[pair]
            first = pl.multiple_of(order[2 * pair] * TILE, TILE)
            second = pl.multiple_of(order[2 * pair + 1] * TILE, TILE)
            left = jnp.concatenate([x[:, pl.ds(first, TILE)], x[:, pl.ds(second, TILE)]], axis=1)
            right = w[pl.ds(2 * pair, 2)].reshape(2 * TILE, A_PER * TILE)
            acc[s] += jnp.dot(left, right, preferred_element_type=jnp.float32)
        return 0

    lax.fori_loop(0, STEPS, step, 0)

    def encode(s, _):
        for r in range(A_PER):
            put_codes(out.at[r, s], acc[s, :, r * TILE : (r + 1) * TILE])
        return 0

    lax.fori_loop(0, SECTORS, encode, 0)


def ladder_codes(order, pair_sector, x, w):
    return pl.pallas_call(
        ladder_kernel,
        in_specs=[
            pl.BlockSpec(memory_space=pltpu.SMEM),
            pl.BlockSpec(memory_space=pltpu.SMEM),
            pl.BlockSpec(memory_space=pl.ANY),
            pl.BlockSpec(memory_space=pl.ANY),
        ],
        out_specs=pl.BlockSpec(memory_space=pltpu.VMEM),
        scratch_shapes=[
            pltpu.VMEM((ROWS, SLOTS * TILE), jnp.bfloat16),
            pltpu.VMEM((PAD_SLOTS, TILE, A_PER * TILE), jnp.bfloat16),
            pltpu.VMEM((SECTORS, ROWS, A_PER * TILE), jnp.float32),
            pltpu.SemaphoreType.DMA,
            pltpu.SemaphoreType.DMA((STEPS,)),
        ],
        out_shape=jax.ShapeDtypeStruct((A_PER, SECTORS, CODE_ROWS, TILE), jnp.int16),
        compiler_params=pltpu.CompilerParams(vmem_limit_bytes=58 * 2**20),
        cost_estimate=pl.CostEstimate(flops=2 * 36 * 256 * 256 * 512, bytes_accessed=16 * 2**20, transcendentals=0),
        name="ladder_codes",
    )(order, pair_sector, x, w)


def recode_kernel(codes, out):
    def one(s, _):
        put_codes(out.at[s], sum(get_codes(codes.at[i, s]) for i in range(A_PER)))
        return 0

    lax.fori_loop(0, SECTORS, one, 0)


def recode(codes):
    return pl.pallas_call(
        recode_kernel,
        out_shape=jax.ShapeDtypeStruct((SECTORS, CODE_ROWS, TILE), jnp.int16),
        compiler_params=pltpu.CompilerParams(vmem_limit_bytes=16 * 2**20),
        name="recode",
    )(codes)


def total_kernel(codes, out):
    out[...] = sum(get_codes(codes.at[i]) for i in range(SECTORS)).astype(jnp.bfloat16)


def total(codes):
    return pl.pallas_call(total_kernel, out_shape=jax.ShapeDtypeStruct((ROWS, TILE), jnp.bfloat16), name="total", compiler_params=pltpu.CompilerParams(vmem_limit_bytes=16 * 2**20))(codes)


def on_device(amplitudes, integrals, out_tile, cd_slot):
    y, c = lax.axis_index("y"), lax.axis_index("c")
    order, valid, place, pair_sector = tables(out_tile[0], cd_slot[0], y, c)
    mine = integrals[0]
    same_core = [mine] + [lax.ppermute(mine, "y", [(i, (i + d) % 4) for i in range(4)]) for d in (1, 2, 3)]
    same_core = jnp.concatenate(same_core, axis=0)
    other_core = lax.ppermute(same_core, "c", [(0, 1), (1, 0)])
    w = arrange(valid, place, same_core, other_core)
    exchanged = lax.all_to_all(amplitudes, ("x", "z"), split_axis=1, concat_axis=0, tiled=True)
    codes = ladder_codes(order, pair_sector, exchanged, w)
    codes = lax.all_to_all(codes, "x", split_axis=0, concat_axis=0, tiled=True)
    codes = lax.all_to_all(recode(codes), "z", split_axis=0, concat_axis=0, tiled=True)
    return total(codes)


def solution(mesh):
    grid = Mesh(mesh.devices.reshape(4, 2, 4, 8), ("y", "c", "x", "z"))
    blk, wide = ("y", "c"), ("x", "z")
    in_specs = (P(blk + wide, None), P(wide, blk, None, None), P(wide, None), P(wide, None))
    return jax.shard_map(on_device, mesh=grid, in_specs=in_specs, out_specs=P(blk, wide), check_vma=False)
```

```python
import jax
import jax.numpy as jnp
from jax import lax
from jax.experimental import pallas as pl
from jax.experimental.pallas import tpu as pltpu
from jax.sharding import Mesh
from jax.sharding import PartitionSpec as P

SECTORS = 8
A_PER = 4
TILE = 128
SLOTS = 64
ENTRIES = SLOTS * A_PER
PAIRS = (SLOTS + SECTORS) // 2
PAD_SLOTS = 2 * PAIRS
ROWS = 256
CODE_ROWS = ROWS + 8
STEP_PAIRS = 9
STEPS = PAIRS // STEP_PAIRS
AHEAD = 2
NEAR = 8
FAR = 4
TOP = 32760.0
TINY = 1e-30
GRAIN = 64.0


def tables(out_tile, cd_slot, y, c):
    entry = jnp.arange(ENTRIES, dtype=jnp.int32)
    key = cd_slot * A_PER + out_tile // SECTORS
    hit = key[None, :] == entry[:, None]
    where_entry = jnp.sum(jnp.where(hit, entry[None, :], 0), axis=1)
    source = where_entry // (ENTRIES // 8)
    hop = (y - source // 2) % 4
    other = jnp.where(source % 2 == c, 0, 1)
    place = ((other * 4 + hop) * (ENTRIES // 8) + where_entry % (ENTRIES // 8)).reshape(SLOTS, A_PER)
    sector = jnp.sum(jnp.where(hit, out_tile[None, :] % SECTORS, 0), axis=1).reshape(SLOTS, A_PER)[:, 0]
    slot = jnp.arange(SLOTS, dtype=jnp.int32)
    of_sector = sector[None, :] == jnp.arange(SECTORS, dtype=jnp.int32)[:, None]
    padded = (jnp.sum(of_sector.astype(jnp.int32), axis=1) + 1) // 2 * 2
    before = jnp.arange(SECTORS)[None, :] < jnp.arange(SECTORS)[:, None]
    start = jnp.sum(jnp.where(before, padded[None, :], 0), axis=1)
    earlier = (sector[None, :] == sector[:, None]) & (slot[None, :] < slot[:, None])
    rank = jnp.sum(earlier.astype(jnp.int32), axis=1)
    position = jnp.sum(jnp.where(of_sector, start[:, None], 0), axis=0) + rank
    at = position[None, :] == jnp.arange(PAD_SLOTS, dtype=jnp.int32)[:, None]
    valid = jnp.sum(at.astype(jnp.int32), axis=1)
    order = jnp.sum(jnp.where(at, slot[None, :], 0), axis=1)
    order_place = jnp.sum(jnp.where(at[:, :, None], place[None, :, :], 0), axis=1)
    pair_first = 2 * jnp.arange(PAIRS, dtype=jnp.int32)
    pair_sector = jnp.sum((start[None, :] <= pair_first[:, None]).astype(jnp.int32), axis=1) - 1
    return order, valid, order_place.reshape(-1), pair_sector


def arrange_kernel(valid, place, same_core, other_core, out, held, sem):
    j = pl.program_id(0)

    @pl.when(j == 0)
    def _():
        half = ENTRIES // 2
        one = pltpu.make_async_copy(same_core, held.at[:half], sem.at[0])
        two = pltpu.make_async_copy(other_core, held.at[half:], sem.at[1])
        one.start()
        two.start()
        one.wait()
        two.wait()

    for i in range(2 * STEP_PAIRS):
        at = j * 2 * STEP_PAIRS + i

        @pl.when(valid[at] == 1)
        def _():
            for r in range(A_PER):
                out[i, :, r * TILE : (r + 1) * TILE] = held[place[at * A_PER + r]]

        @pl.when(valid[at] == 0)
        def _():
            out[i] = jnp.zeros((TILE, A_PER * TILE), out.dtype)


def arrange(valid, place, same_core, other_core):
    return pl.pallas_call(
        arrange_kernel,
        grid_spec=pltpu.PrefetchScalarGridSpec(
            num_scalar_prefetch=2,
            grid=(STEPS,),
            in_specs=[pl.BlockSpec(memory_space=pl.ANY)] * 2,
            out_specs=pl.BlockSpec((2 * STEP_PAIRS, TILE, A_PER * TILE), lambda j, v, p: (j, 0, 0)),
            scratch_shapes=[
                pltpu.VMEM((ENTRIES, TILE, TILE), jnp.bfloat16),
                pltpu.SemaphoreType.DMA((2,)),
            ],
        ),
        out_shape=jax.ShapeDtypeStruct((PAD_SLOTS, TILE, A_PER * TILE), jnp.bfloat16),
        cost_estimate=pl.CostEstimate(flops=0, bytes_accessed=2 * 9 * 2**20, transcendentals=0),
        name="arrange",
    )(valid, place, same_core, other_core)


def put_codes(out, v):
    top = jnp.maximum(jnp.max(jnp.abs(v), axis=0, keepdims=True), TINY)
    level = jnp.ceil(jnp.log2(top) * GRAIN + 1.0)
    factor = TOP * jnp.exp2(-level * (1.0 / GRAIN))
    out[:ROWS, :] = jnp.round(v * factor).astype(jnp.int32).astype(jnp.int16)
    out[ROWS:, :] = jnp.broadcast_to(level.astype(jnp.int32), (CODE_ROWS - ROWS, TILE)).astype(jnp.int16)


def get_codes(codes):
    level = codes[ROWS:, :].astype(jnp.int32).astype(jnp.float32)[:1]
    scale = jnp.exp2(level * (1.0 / GRAIN)) * (1.0 / TOP)
    return codes[:ROWS, :].astype(jnp.int32).astype(jnp.float32) * scale


def ladder_kernel(order, pair_sector, x_hbm, w_hbm, out, x, w, acc, x_sem, w_sem):
    x_copy = pltpu.make_async_copy(x_hbm, x, x_sem)
    x_copy.start()

    def w_copy(k):
        part = pl.ds(k * 2 * STEP_PAIRS, 2 * STEP_PAIRS)
        return pltpu.make_async_copy(w_hbm.at[part], w.at[part], w_sem.at[k])

    for k in range(AHEAD):
        w_copy(k).start()
    acc[...] = jnp.zeros_like(acc)
    x_copy.wait()

    def step(k, _):
        @pl.when(k + AHEAD < STEPS)
        def _():
            w_copy(k + AHEAD).start()

        w_copy(k).wait()
        for i in range(STEP_PAIRS):
            pair = k * STEP_PAIRS + i
            s = pair_sector[pair]
            first = pl.multiple_of(order[2 * pair] * TILE, TILE)
            second = pl.multiple_of(order[2 * pair + 1] * TILE, TILE)
            left = jnp.concatenate([x[:, pl.ds(first, TILE)], x[:, pl.ds(second, TILE)]], axis=1)
            right = w[pl.ds(2 * pair, 2)].reshape(2 * TILE, A_PER * TILE)
            acc[s] += jnp.dot(left, right, preferred_element_type=jnp.float32)
        return 0

    lax.fori_loop(0, STEPS, step, 0)

    def encode(s, _):
        for r in range(A_PER):
            put_codes(out.at[r * 2 + s % 2, s // 2], acc[s, :, r * TILE : (r + 1) * TILE])
        return 0

    lax.fori_loop(0, SECTORS, encode, 0)


def ladder_codes(order, pair_sector, x, w):
    return pl.pallas_call(
        ladder_kernel,
        in_specs=[
            pl.BlockSpec(memory_space=pltpu.SMEM),
            pl.BlockSpec(memory_space=pltpu.SMEM),
            pl.BlockSpec(memory_space=pl.ANY),
            pl.BlockSpec(memory_space=pl.ANY),
        ],
        out_specs=pl.BlockSpec(memory_space=pltpu.VMEM),
        scratch_shapes=[
            pltpu.VMEM((ROWS, SLOTS * TILE), jnp.bfloat16),
            pltpu.VMEM((PAD_SLOTS, TILE, A_PER * TILE), jnp.bfloat16),
            pltpu.VMEM((SECTORS, ROWS, A_PER * TILE), jnp.float32),
            pltpu.SemaphoreType.DMA,
            pltpu.SemaphoreType.DMA((STEPS,)),
        ],
        out_shape=jax.ShapeDtypeStruct((NEAR, FAR, CODE_ROWS, TILE), jnp.int16),
        compiler_params=pltpu.CompilerParams(vmem_limit_bytes=58 * 2**20),
        cost_estimate=pl.CostEstimate(flops=2 * 36 * 256 * 256 * 512, bytes_accessed=16 * 2**20, transcendentals=0),
        name="ladder_codes",
    )(order, pair_sector, x, w)


def recode_kernel(codes, out):
    def one(s, _):
        put_codes(out.at[s], sum(get_codes(codes.at[i, s]) for i in range(NEAR)))
        return 0

    lax.fori_loop(0, FAR, one, 0)


def recode(codes):
    return pl.pallas_call(
        recode_kernel,
        out_shape=jax.ShapeDtypeStruct((FAR, CODE_ROWS, TILE), jnp.int16),
        compiler_params=pltpu.CompilerParams(vmem_limit_bytes=16 * 2**20),
        name="recode",
    )(codes)


def total_kernel(codes, out):
    out[...] = sum(get_codes(codes.at[i]) for i in range(FAR)).astype(jnp.bfloat16)


def total(codes):
    return pl.pallas_call(total_kernel, out_shape=jax.ShapeDtypeStruct((ROWS, TILE), jnp.bfloat16), name="total", compiler_params=pltpu.CompilerParams(vmem_limit_bytes=16 * 2**20))(codes)


def on_device(amplitudes, integrals, out_tile, cd_slot):
    y, c = lax.axis_index("y"), lax.axis_index("c")
    order, valid, place, pair_sector = tables(out_tile[0], cd_slot[0], y, c)
    mine = integrals[0]
    same_core = [mine] + [lax.ppermute(mine, "y", [(i, (i + d) % 4) for i in range(4)]) for d in (1, 2, 3)]
    same_core = jnp.concatenate(same_core, axis=0)
    other_core = lax.ppermute(same_core, "c", [(0, 1), (1, 0)])
    w = arrange(valid, place, same_core, other_core)
    exchanged = lax.all_to_all(amplitudes, ("x", "h", "l"), split_axis=1, concat_axis=0, tiled=True)
    codes = ladder_codes(order, pair_sector, exchanged, w)
    codes = lax.all_to_all(codes, ("x", "l"), split_axis=0, concat_axis=0, tiled=True)
    codes = lax.all_to_all(recode(codes), "h", split_axis=0, concat_axis=0, tiled=True)
    return total(codes)


def solution(mesh):
    grid = Mesh(mesh.devices.reshape(4, 2, 4, 4, 2), ("y", "c", "x", "h", "l"))
    blk, wide = ("y", "c"), ("x", "h", "l")
    in_specs = (P(blk + wide, None), P(wide, blk, None, None), P(wide, None), P(wide, None))
    return jax.shard_map(on_device, mesh=grid, in_specs=in_specs, out_specs=P(blk, wide), check_vma=False)
```

```python
import jax
import jax.numpy as jnp
from jax import lax
from jax.experimental import pallas as pl
from jax.experimental.pallas import tpu as pltpu
from jax.sharding import Mesh
from jax.sharding import PartitionSpec as P

SECTORS = 8
A_PER = 4
TILE = 128
SLOTS = 64
ENTRIES = SLOTS * A_PER
PAIRS = (SLOTS + SECTORS) // 2
PAD_SLOTS = 2 * PAIRS
ROWS = 256
CODE_ROWS = ROWS + 8
STEP_PAIRS = 9
STEPS = PAIRS // STEP_PAIRS
AHEAD = 2
NEAR = 8
FAR = 4
TOP = 32760.0
TINY = 1e-30
GRAIN = 64.0


def tables(out_tile, cd_slot, y, c):
    entry = jnp.arange(ENTRIES, dtype=jnp.int32)
    key = cd_slot * A_PER + out_tile // SECTORS
    hit = key[None, :] == entry[:, None]
    where_entry = jnp.sum(jnp.where(hit, entry[None, :], 0), axis=1)
    source = where_entry // (ENTRIES // 8)
    hop = (y - source // 2) % 4
    other = jnp.where(source % 2 == c, 0, 1)
    place = ((other * 4 + hop) * (ENTRIES // 8) + where_entry % (ENTRIES // 8)).reshape(SLOTS, A_PER)
    sector = jnp.sum(jnp.where(hit, out_tile[None, :] % SECTORS, 0), axis=1).reshape(SLOTS, A_PER)[:, 0]
    slot = jnp.arange(SLOTS, dtype=jnp.int32)
    of_sector = sector[None, :] == jnp.arange(SECTORS, dtype=jnp.int32)[:, None]
    padded = (jnp.sum(of_sector.astype(jnp.int32), axis=1) + 1) // 2 * 2
    before = jnp.arange(SECTORS)[None, :] < jnp.arange(SECTORS)[:, None]
    start = jnp.sum(jnp.where(before, padded[None, :], 0), axis=1)
    earlier = (sector[None, :] == sector[:, None]) & (slot[None, :] < slot[:, None])
    rank = jnp.sum(earlier.astype(jnp.int32), axis=1)
    position = jnp.sum(jnp.where(of_sector, start[:, None], 0), axis=0) + rank
    at = position[None, :] == jnp.arange(PAD_SLOTS, dtype=jnp.int32)[:, None]
    valid = jnp.sum(at.astype(jnp.int32), axis=1)
    order = jnp.sum(jnp.where(at, slot[None, :], 0), axis=1)
    order_place = jnp.sum(jnp.where(at[:, :, None], place[None, :, :], 0), axis=1)
    pair_first = 2 * jnp.arange(PAIRS, dtype=jnp.int32)
    pair_sector = jnp.sum((start[None, :] <= pair_first[:, None]).astype(jnp.int32), axis=1) - 1
    return order, valid, order_place.reshape(-1), pair_sector


def arrange_kernel(valid, place, same_core, other_core, out, held, sem):
    j = pl.program_id(0)

    @pl.when(j == 0)
    def _():
        half = ENTRIES // 2
        one = pltpu.make_async_copy(same_core, held.at[:half], sem.at[0])
        two = pltpu.make_async_copy(other_core, held.at[half:], sem.at[1])
        one.start()
        two.start()
        one.wait()
        two.wait()

    for i in range(2 * STEP_PAIRS):
        at = j * 2 * STEP_PAIRS + i

        @pl.when(valid[at] == 1)
        def _():
            for r in range(A_PER):
                out[i, :, r * TILE : (r + 1) * TILE] = held[place[at * A_PER + r]]

        @pl.when(valid[at] == 0)
        def _():
            out[i] = jnp.zeros((TILE, A_PER * TILE), out.dtype)


def arrange(valid, place, same_core, other_core):
    return pl.pallas_call(
        arrange_kernel,
        grid_spec=pltpu.PrefetchScalarGridSpec(
            num_scalar_prefetch=2,
            grid=(STEPS,),
            in_specs=[pl.BlockSpec(memory_space=pl.ANY)] * 2,
            out_specs=pl.BlockSpec((2 * STEP_PAIRS, TILE, A_PER * TILE), lambda j, v, p: (j, 0, 0)),
            scratch_shapes=[
                pltpu.VMEM((ENTRIES, TILE, TILE), jnp.bfloat16),
                pltpu.SemaphoreType.DMA((2,)),
            ],
        ),
        out_shape=jax.ShapeDtypeStruct((PAD_SLOTS, TILE, A_PER * TILE), jnp.bfloat16),
        cost_estimate=pl.CostEstimate(flops=0, bytes_accessed=2 * 9 * 2**20, transcendentals=0),
        name="arrange",
    )(valid, place, same_core, other_core)


def put_codes(out, v):
    top = jnp.maximum(jnp.max(jnp.abs(v), axis=0, keepdims=True), TINY)
    level = jnp.ceil(jnp.log2(top) * GRAIN + 1.0)
    factor = TOP * jnp.exp2(-level * (1.0 / GRAIN))
    out[:ROWS, :] = jnp.round(v * factor).astype(jnp.int32).astype(jnp.int16)
    out[ROWS:, :] = jnp.broadcast_to(level.astype(jnp.int32), (CODE_ROWS - ROWS, TILE)).astype(jnp.int16)


def get_codes(codes):
    level = codes[ROWS:, :].astype(jnp.int32).astype(jnp.float32)[:1]
    scale = jnp.exp2(level * (1.0 / GRAIN)) * (1.0 / TOP)
    return codes[:ROWS, :].astype(jnp.int32).astype(jnp.float32) * scale


def ladder_kernel(order, pair_sector, x_hbm, w_hbm, out, x, w, acc, x_sem, w_sem):
    x_copy = pltpu.make_async_copy(x_hbm, x, x_sem)
    x_copy.start()

    def w_copy(k):
        part = pl.ds(k * 2 * STEP_PAIRS, 2 * STEP_PAIRS)
        return pltpu.make_async_copy(w_hbm.at[part], w.at[part], w_sem.at[k])

    for k in range(AHEAD):
        w_copy(k).start()
    acc[...] = jnp.zeros_like(acc)
    x_copy.wait()

    def step(k, _):
        @pl.when(k + AHEAD < STEPS)
        def _():
            w_copy(k + AHEAD).start()

        w_copy(k).wait()
        for i in range(STEP_PAIRS):
            pair = k * STEP_PAIRS + i
            s = pair_sector[pair]
            first = pl.multiple_of(order[2 * pair] * TILE, TILE)
            second = pl.multiple_of(order[2 * pair + 1] * TILE, TILE)
            left = jnp.concatenate([x[:, pl.ds(first, TILE)], x[:, pl.ds(second, TILE)]], axis=1)
            right = w[pl.ds(2 * pair, 2)].reshape(2 * TILE, A_PER * TILE)
            acc[s] += jnp.dot(left, right, preferred_element_type=jnp.float32)
        return 0

    lax.fori_loop(0, STEPS, step, 0)

    def encode(s, _):
        for r in range(A_PER):
            put_codes(out.at[r * 2 + s % 2, s // 2], acc[s, :, r * TILE : (r + 1) * TILE])
        return 0

    lax.fori_loop(0, SECTORS, encode, 0)


def ladder_codes(order, pair_sector, x, w):
    return pl.pallas_call(
        ladder_kernel,
        in_specs=[
            pl.BlockSpec(memory_space=pltpu.SMEM),
            pl.BlockSpec(memory_space=pltpu.SMEM),
            pl.BlockSpec(memory_space=pl.ANY),
            pl.BlockSpec(memory_space=pl.ANY),
        ],
        out_specs=pl.BlockSpec(memory_space=pltpu.VMEM),
        scratch_shapes=[
            pltpu.VMEM((ROWS, SLOTS * TILE), jnp.bfloat16),
            pltpu.VMEM((PAD_SLOTS, TILE, A_PER * TILE), jnp.bfloat16),
            pltpu.VMEM((SECTORS, ROWS, A_PER * TILE), jnp.float32),
            pltpu.SemaphoreType.DMA,
            pltpu.SemaphoreType.DMA((STEPS,)),
        ],
        out_shape=jax.ShapeDtypeStruct((NEAR, FAR, CODE_ROWS, TILE), jnp.int16),
        compiler_params=pltpu.CompilerParams(vmem_limit_bytes=44 * 2**20),
        cost_estimate=pl.CostEstimate(flops=2 * 36 * 256 * 256 * 512, bytes_accessed=16 * 2**20, transcendentals=0),
        name="ladder_codes",
    )(order, pair_sector, x, w)


def recode_kernel(codes, out):
    def one(s, _):
        put_codes(out.at[s], sum(get_codes(codes.at[i, s]) for i in range(NEAR)))
        return 0

    lax.fori_loop(0, FAR, one, 0)


def recode(codes):
    return pl.pallas_call(
        recode_kernel,
        out_shape=jax.ShapeDtypeStruct((FAR, CODE_ROWS, TILE), jnp.int16),
        compiler_params=pltpu.CompilerParams(vmem_limit_bytes=16 * 2**20),
        name="recode",
    )(codes)


def total_kernel(codes, out):
    out[...] = sum(get_codes(codes.at[i]) for i in range(FAR)).astype(jnp.bfloat16)


def total(codes):
    return pl.pallas_call(total_kernel, out_shape=jax.ShapeDtypeStruct((ROWS, TILE), jnp.bfloat16), name="total", compiler_params=pltpu.CompilerParams(vmem_limit_bytes=16 * 2**20))(codes)


def on_device(amplitudes, integrals, out_tile, cd_slot):
    y, c = lax.axis_index("y"), lax.axis_index("c")
    order, valid, place, pair_sector = tables(out_tile[0], cd_slot[0], y, c)
    mine = integrals[0]
    same_core = [mine] + [lax.ppermute(mine, "y", [(i, (i + d) % 4) for i in range(4)]) for d in (1, 2, 3)]
    same_core = jnp.concatenate(same_core, axis=0)
    other_core = lax.ppermute(same_core, "c", [(0, 1), (1, 0)])
    w = arrange(valid, place, same_core, other_core)
    exchanged = lax.all_to_all(amplitudes, ("x", "h", "l"), split_axis=1, concat_axis=0, tiled=True)
    codes = ladder_codes(order, pair_sector, exchanged, w)
    codes = lax.all_to_all(codes, ("x", "l"), split_axis=0, concat_axis=0, tiled=True)
    codes = lax.all_to_all(recode(codes), "h", split_axis=0, concat_axis=0, tiled=True)
    return total(codes)


def solution(mesh):
    grid = Mesh(mesh.devices.reshape(4, 2, 4, 4, 2), ("y", "c", "x", "h", "l"))
    blk, wide = ("y", "c"), ("x", "h", "l")
    in_specs = (P(blk + wide, None), P(wide, blk, None, None), P(wide, None), P(wide, None))
    return jax.shard_map(on_device, mesh=grid, in_specs=in_specs, out_specs=P(blk, wide), check_vma=False)
```
